1024 devices in a mesh: seq: 32 (over y_lo, z), chan: 32 (over x, y_hi, core).
Axes of the slice: x: 8, y: 8 (y_hi: 2, y_lo: 4; y = y_hi * 4 + y_lo), z: 8, core: 2. Of those that a mesh axis runs over, the one named last changes fastest.
Arguments:
- query_proj: bfloat16 [4096, 8192], P('seq', 'chan'), may hold values from -18 to 18
- key_proj: bfloat16 [4096, 8192], P('seq', 'chan'), may hold values from -6 to 6
- value_proj: bfloat16 [4096, 8192], P('seq', 'chan'), may hold values from -6 to 6
- filters: bfloat16 [8192, 4096], P('chan', 'seq'), may hold values from -48 to 48
- norm_gain: float32 [8192], P('chan'), may hold values from 0.25 to 1.75
- out_grad: bfloat16 [4096, 8192], P('seq', 'chan'), may hold values from -6 to 6
Outputs:
- normed: bfloat16 [4096, 8192], P('seq', 'chan')
- query_grad: bfloat16 [4096, 8192], P('seq', 'chan')
- key_grad: bfloat16 [4096, 8192], P('seq', 'chan')
- value_grad: bfloat16 [4096, 8192], P('seq', 'chan')
The draws below stay inside these ranges and needn't reach their ends.
All inputs are finite; a program needn't handle non-finite values.
Results may differ from the reference program's by a relative error of at most 0.0095.
Values may be sent and summed in bfloat16 or wider, within the bound.
No kernel may reach another device: no remote copies, remote signals or barrier semaphores. Data moves between devices by JAX's collectives and lax.ppermute only.
A program may use at most 32 MiB of HBM per device.

```python
import math
import jax
import jax.numpy as jnp
from jax import lax

D = 8192
SEQ_LEN = 4096


def draw_query_proj(key, part):
    first_key, second_key = jax.random.split(key)
    row_scale = jnp.exp(jax.random.uniform(first_key, (SEQ_LEN, 1), jnp.float32, math.log(0.3), math.log(3.0)))
    noise = jnp.clip(jax.random.normal(second_key, (SEQ_LEN, D), jnp.float32), -6.0, 6.0)
    return (noise * row_scale).astype(jnp.bfloat16)


def draw_filters(key, part):
    first_key, second_key, third_key = jax.random.split(key, 3)
    channel = jnp.arange(D, dtype=jnp.float32) / max(D - 1, 1)
    base = jnp.exp(jax.random.uniform(first_key, (D, 1), jnp.float32, math.log(0.4), math.log(4.0)))
    reach = jnp.exp(jax.random.uniform(second_key, (D, 1), jnp.float32, math.log(32.0), math.log(2.0 * SEQ_LEN)))
    ramp = 1.0 + channel
    noise = jnp.clip(jax.random.normal(third_key, (D, SEQ_LEN), jnp.float32), -6.0, 6.0)
    positions = jnp.arange(SEQ_LEN, dtype=jnp.float32)[None, :]
    envelope = jnp.exp(-positions / reach)
    norms = jnp.sqrt(jnp.sum(envelope * envelope, axis=1, keepdims=True))
    return (noise * envelope / norms * base * ramp[:, None]).astype(jnp.bfloat16)


def steps_of(key, shape, cuts, low, high):
    loudness = 1.0
    for axis_at, parts in cuts:
        heights = jax.random.uniform(jax.random.fold_in(jax.random.fold_in(key, 6), axis_at), (parts,), jnp.float32, low / len(cuts), high / len(cuts))
        loudness = loudness * jnp.repeat(jnp.exp(heights), shape[axis_at] // parts).reshape((-1,) + (1,) * (len(shape) - 1 - axis_at))
    return loudness


def scatter_about(key, shape, width, bound, cuts=(), kind=jnp.bfloat16):
    entries = jax.random.normal(key, shape, jnp.float32) * width
    if len(cuts) > 0:
        entries = steps_of(key, shape, cuts, -0.22, 0.18) * entries
    return jnp.clip(entries, min=-bound, max=bound).astype(kind)


def setup_inputs(seed: int = 0) -> dict:
    key_list = jax.random.split(jax.random.key(seed), 7)
    return {
        "query_proj": draw_query_proj(jax.random.fold_in(key_list[6], 71), 0),
        "key_proj": scatter_about(key_list[1], (SEQ_LEN, D), 1.0, 6.0, ((0, 32), (1, 32))),
        "value_proj": scatter_about(key_list[2], (SEQ_LEN, D), 1.0, 6.0, ((0, 32), (1, 32))),
        "filters": draw_filters(jax.random.fold_in(key_list[6], 71), 0),
        "norm_gain": jnp.clip(1.0 + 0.15 * jax.random.normal(key_list[4], (D,), jnp.float32), 0.25, 1.75),
        "out_grad": scatter_about(key_list[5], (SEQ_LEN, D), 1.0, 6.0, ((0, 32), (1, 32))),
    }


EPSILON = 1e-05

def rounded(array):
    return lax.optimization_barrier(array.astype(jnp.bfloat16)).astype(jnp.float32)

def forward_block(pieces):
    query_blk, key_blk, value_blk, filter_blk = pieces
    extent = 2 * SEQ_LEN
    source = rounded(key_blk.astype(jnp.float32) * value_blk.astype(jnp.float32))
    kernel = jnp.fft.rfft(filter_blk.astype(jnp.float32), n=extent, axis=1)
    convolved = jnp.fft.irfft(jnp.fft.rfft(source, n=extent, axis=1) * kernel, n=extent, axis=1)[:, :SEQ_LEN]
    convolved = convolved.astype(jnp.bfloat16)
    product = (query_blk.astype(jnp.float32) * convolved.astype(jnp.float32)).astype(jnp.bfloat16)
    return (product, convolved)

def backward_block(pieces):
    grad_blk, query_blk, key_blk, value_blk, filter_blk, convolved = pieces
    extent = 2 * SEQ_LEN
    grad_wide = grad_blk.astype(jnp.float32)
    query_grad = (grad_wide * convolved.astype(jnp.float32)).astype(jnp.bfloat16)
    weighted = rounded(grad_wide * query_blk.astype(jnp.float32))
    kernel = jnp.fft.rfft(filter_blk.astype(jnp.float32), n=extent, axis=1)
    spread = jnp.fft.irfft(jnp.fft.rfft(weighted, n=extent, axis=1) * jnp.conj(kernel), n=extent, axis=1)[:, :SEQ_LEN]
    spread = rounded(spread)
    key_grad = (spread * value_blk.astype(jnp.float32)).astype(jnp.bfloat16)
    value_grad = (spread * key_blk.astype(jnp.float32)).astype(jnp.bfloat16)
    return (query_grad, key_grad, value_grad)

def reference(query_proj, key_proj, value_proj, filters, norm_gain, out_grad):
    grouping = min(D, 256)
    count = D // grouping

    def blocks(array):
        return array.T.reshape(count, grouping, SEQ_LEN)

    def tokens(array):
        return array.reshape(D, SEQ_LEN).T
    query_b = blocks(query_proj)
    key_b = blocks(key_proj)
    value_b = blocks(value_proj)
    dout_b = blocks(out_grad)
    filter_b = filters.reshape(count, grouping, SEQ_LEN)
    gain_b = norm_gain.reshape(count, grouping, 1)
    product, convolved = lax.map(forward_block, (query_b, key_b, value_b, filter_b))
    product = lax.optimization_barrier(product)
    prod_wide = product.astype(jnp.float32)
    square_sum = lax.optimization_barrier(jnp.sum(prod_wide * prod_wide, axis=(0, 1)))
    scale = lax.rsqrt(square_sum / D + EPSILON)
    normed = (prod_wide * scale * gain_b).astype(jnp.bfloat16)
    gained = dout_b.astype(jnp.float32) * gain_b
    cross_sum = lax.optimization_barrier(jnp.sum(gained * prod_wide, axis=(0, 1)))
    grad_product = (gained * scale - prod_wide * (cross_sum * scale * scale * scale / D)).astype(jnp.bfloat16)
    grad_product = lax.optimization_barrier(grad_product)
    query_grad, key_grad, value_grad = lax.map(backward_block, (grad_product, query_b, key_b, value_b, filter_b, convolved))
    return (tokens(normed), tokens(query_grad), tokens(key_grad), tokens(value_grad))
```

```python
import functools

import jax
import jax.numpy as jnp
import numpy as np
from jax import lax
from jax.experimental import pallas as pl
from jax.experimental.pallas import tpu as pltpu
from jax.sharding import PartitionSpec as P

D = 8192
EPSILON = 1e-05

BF16 = jnp.bfloat16
F32 = jnp.float32


def split_halves(table):
    high = table.astype(jnp.bfloat16)
    low = (table - high.astype(np.float64)).astype(jnp.bfloat16)
    return (high, low)


def make_tables(blocks, block, rows):
    length = blocks * block
    n1 = np.arange(blocks)
    k1 = np.arange(blocks)
    outer = np.exp(-2j * np.pi * np.outer(k1 + 0.25, n1) / blocks)
    stacked = np.concatenate([outer.real, outer.imag], axis=0)
    eye = np.eye(rows)
    first = np.kron(stacked, eye)
    last = np.kron(stacked.T, eye) / length
    twist = np.exp(-2j * np.pi * np.outer(k1 + 0.25, np.arange(block)) / length)
    twist = np.repeat(twist, rows, axis=0)
    angle = 2 * np.pi * (np.outer(np.arange(block), np.arange(block)) % block) / block
    inner = np.block([[np.cos(angle), -np.sin(angle)], [np.sin(angle), np.cos(angle)]])
    first_high, first_low = split_halves(first)
    last_high, last_low = split_halves(last)
    inner_high, inner_low = split_halves(inner)
    return {
        "first": np.stack([first_high, first_low]),
        "last": np.stack([last_high, last_low]),
        "inner": np.stack([inner_high, inner_low]),
        "twist": np.stack([twist.real, twist.imag]).astype(np.float32),
    }


def halves(wide):
    high = wide.astype(BF16)
    low = (wide - high.astype(F32)).astype(BF16)
    return (high, low)


def mul(left, right, flip=False):
    dims = (((1,), (1 if flip else 0,)), ((), ()))
    return lax.dot_general(left, right, dims, preferred_element_type=F32)


def to_values(signal, first, inner, twist):
    rows, width = signal.shape
    block = twist.shape[2]
    part = mul(first[0], signal) + mul(first[1], signal)
    turned = []
    for i in range(width // block):
        part_re = part[:rows, i * block : (i + 1) * block]
        part_im = part[rows:, i * block : (i + 1) * block]
        turned.append(
            jnp.concatenate(
                [part_re * twist[0] - part_im * twist[1], part_re * twist[1] + part_im * twist[0]],
                axis=1,
            )
        )
    high, low = halves(jnp.concatenate(turned, axis=0))
    values = mul(high, inner[0]) + (mul(high, inner[1]) + mul(low, inner[0]))
    return [
        (values[i * rows : (i + 1) * rows, :block], values[i * rows : (i + 1) * rows, block:])
        for i in range(width // block)
    ]


def to_signal(value_re, value_im, last, inner, twist):
    block = twist.shape[2]
    high, low = halves(jnp.concatenate([value_re, value_im], axis=1))
    back = mul(high, inner[0], True) + (mul(high, inner[1], True) + mul(low, inner[0], True))
    back_re, back_im = back[:, :block], back[:, block:]
    turned = jnp.concatenate(
        [back_re * twist[0] + back_im * twist[1], back_im * twist[0] - back_re * twist[1]], axis=0
    )
    high, low = halves(turned)
    return mul(last[0], high) + (mul(last[0], low) + mul(last[1], high))


def call(body, outs, *args, name):
    shapes = [jax.ShapeDtypeStruct(shape, dtype) for shape, dtype in outs]
    return pl.pallas_call(body, out_shape=shapes, name=name)(*args)


def source_body(key_ref, value_ref, filter_ref, out_ref):
    peers, double, block = out_ref.shape
    source = (key_ref[...].astype(F32) * value_ref[...].astype(F32)).astype(BF16).astype(F32)
    source = source.T.reshape(peers, double // 2, block)
    taps = filter_ref[...].astype(F32).reshape(peers, double // 2, block)
    out_ref[...] = jnp.concatenate([source, taps], axis=1).astype(BF16)


def turn_body(query_ref, grad_ref, gain_ref, query_out, gained_out):
    query_out[...] = query_ref[...].astype(F32).T.astype(BF16)
    gained_out[...] = (grad_ref[...].astype(F32) * gain_ref[...]).T


def convolve_body(packed_ref, first_ref, last_ref, inner_ref, twist_ref, out_ref, values_ref):
    peers, double, block = packed_ref.shape
    per = double // 2
    packed = packed_ref[...].astype(F32)
    source = packed[:, :per].reshape(peers * per, block)
    taps = packed[:, per:].reshape(peers * per, block)
    signal = jnp.concatenate([source, taps], axis=1).astype(BF16)
    (src_re, src_im), (tap_re, tap_im) = to_values(signal, first_ref, inner_ref, twist_ref)
    values_ref[0] = tap_re
    values_ref[1] = tap_im
    out = to_signal(
        src_re * tap_re - src_im * tap_im,
        src_re * tap_im + src_im * tap_re,
        last_ref,
        inner_ref,
        twist_ref,
    )
    out_ref[...] = out.reshape(peers, per, block).astype(BF16)


def correlate_body(
    weighted_ref, values_ref, first_ref, last_ref, inner_ref, twist_ref, out_ref
):
    peers, per, block = weighted_ref.shape
    signal = weighted_ref[...].astype(F32).reshape(peers * per, block).astype(BF16)
    ((sig_re, sig_im),) = to_values(signal, first_ref, inner_ref, twist_ref)
    tap_re, tap_im = values_ref[0], values_ref[1]
    out = to_signal(
        sig_re * tap_re + sig_im * tap_im,
        sig_im * tap_re - sig_re * tap_im,
        last_ref,
        inner_ref,
        twist_ref,
    )
    out_ref[...] = out.reshape(peers, per, block).astype(BF16)


def product_of(conv_ref, query_ref):
    peers, per, block = conv_ref.shape
    conv = conv_ref[...].astype(F32).reshape(peers * per, block)
    query = query_ref[...].astype(F32)
    return (conv, query, (query * conv).astype(BF16).astype(F32))


def partial_body(conv_ref, query_ref, gained_ref, out_ref):
    _, _, product = product_of(conv_ref, query_ref)
    square = jnp.sum(product * product, axis=0, keepdims=True)
    cross = jnp.sum(gained_ref[...] * product, axis=0, keepdims=True)
    both = jnp.concatenate([square, cross], axis=0)
    out_ref[...] = jnp.broadcast_to(both[None], out_ref.shape)


def token_scales(sums_ref, width):
    sums = jnp.sum(sums_ref[...], axis=0)
    scale = lax.rsqrt(sums[0:1] / width + EPSILON)
    return (scale, sums[1:2] * scale * scale * scale / width)


def weighted_body(sums_ref, conv_ref, query_ref, gained_ref, weighted_ref, grad_ref, *, width):
    scale, pull = token_scales(sums_ref, width)
    _, query, product = product_of(conv_ref, query_ref)
    grad = (gained_ref[...] * scale - product * pull).astype(BF16)
    grad_ref[...] = grad
    weighted = grad.astype(F32) * query
    weighted_ref[...] = weighted.reshape(weighted_ref.shape).astype(BF16)


def outputs_body(
    sums_ref, conv_ref, query_ref, grad_ref, gain_ref, normed_ref, query_grad_ref, *, width
):
    scale, _ = token_scales(sums_ref, width)
    conv, _, product = product_of(conv_ref, query_ref)
    normed_ref[...] = ((product * scale).T * gain_ref[...]).astype(BF16)
    query_grad_ref[...] = (grad_ref[...].astype(F32) * conv).T.astype(BF16)


def finish_body(spread_ref, key_ref, value_ref, key_grad_ref, value_grad_ref):
    peers, per, block = spread_ref.shape
    spread = spread_ref[...].astype(F32).reshape(peers * per, block).T
    key_grad_ref[...] = (spread * value_ref[...].astype(F32)).astype(BF16)
    value_grad_ref[...] = (spread * key_ref[...].astype(F32)).astype(BF16)


def per_device(query, key, value, filters, gain, out_grad):
    peers = lax.axis_size("seq")
    groups = lax.axis_size("chan")
    block, wide = query.shape
    per = wide // peers
    width = float(wide * groups)
    tables = make_tables(peers, block, per)
    first, last, inner, twist = (
        jnp.asarray(tables[name]) for name in ("first", "last", "inner", "twist")
    )
    gain = gain.reshape(1, wide)

    def exchange(array, axis="seq"):
        return lax.all_to_all(array, axis, split_axis=0, concat_axis=0, tiled=True)

    (packed,) = call(
        source_body, [((peers, 2 * per, block), BF16)], key, value, filters, name="source"
    )
    packed = exchange(packed)
    query_t, gained_t = call(
        turn_body, [((wide, block), BF16), ((wide, block), F32)], query, out_grad, gain, name="turn"
    )
    conv, values = call(
        convolve_body,
        [((peers, per, block), BF16), ((2, wide, block), F32)],
        packed,
        first,
        last,
        inner,
        twist,
        name="convolve",
    )
    conv = exchange(conv)
    (partial,) = call(
        partial_body, [((groups, 2, block), F32)], conv, query_t, gained_t, name="partial"
    )
    sums = exchange(partial, "chan")
    weighted, grad = call(
        functools.partial(weighted_body, width=width),
        [((peers, per, block), BF16), ((wide, block), BF16)],
        sums,
        conv,
        query_t,
        gained_t,
        name="weighted",
    )
    weighted = exchange(weighted)
    normed, query_grad = call(
        functools.partial(outputs_body, width=width),
        [((block, wide), BF16), ((block, wide), BF16)],
        sums,
        conv,
        query_t,
        grad,
        gain,
        name="outputs",
    )
    (spread,) = call(
        correlate_body,
        [((peers, per, block), BF16)],
        weighted,
        values,
        first,
        last,
        inner,
        twist,
        name="correlate",
    )
    spread = exchange(spread)
    key_grad, value_grad = call(
        finish_body,
        [((block, wide), BF16), ((block, wide), BF16)],
        spread,
        key,
        value,
        name="finish",
    )
    return (normed, query_grad, key_grad, value_grad)


def solution(mesh):
    tokens = P("seq", "chan")
    return jax.shard_map(
        per_device,
        mesh=mesh,
        in_specs=(tokens, tokens, tokens, P("chan", "seq"), P("chan"), tokens),
        out_specs=(tokens, tokens, tokens, tokens),
        check_vma=False,
    )
```

```python
import functools

import jax
import jax.numpy as jnp
import numpy as np
from jax import lax
from jax.experimental import pallas as pl
from jax.experimental.pallas import tpu as pltpu
from jax.sharding import PartitionSpec as P

D = 8192
EPSILON = 1e-05

BF16 = jnp.bfloat16
F32 = jnp.float32
VMEM_LIMIT = 24 << 20


def split_halves(table):
    high = table.astype(jnp.bfloat16)
    low = (table - high.astype(np.float64)).astype(jnp.bfloat16)
    return [high, low]


def make_table(blocks, block, rows):
    length = blocks * block
    steps = np.arange(blocks)
    outer = np.exp(-2j * np.pi * np.outer(steps + 0.25, steps) / blocks)
    eye = np.eye(rows)
    first = np.kron(np.concatenate([outer.real, outer.imag], axis=0), eye)
    last = [np.kron(part.T, eye) / length for part in (outer.real, outer.imag)]
    twist = np.exp(-2j * np.pi * np.outer(steps + 0.25, np.arange(block)) / length)
    twist = np.repeat(np.concatenate([twist.real, twist.imag], axis=1), rows, axis=0)
    angle = 2 * np.pi * (np.outer(np.arange(block), np.arange(block)) % block) / block
    inner = np.block([[np.cos(angle), -np.sin(angle)], [np.sin(angle), np.cos(angle)]])
    parts = split_halves(first) + split_halves(inner) + split_halves(twist)
    parts = parts + split_halves(last[0]) + split_halves(last[1])
    return np.concatenate(parts, axis=0)


class Table:
    def __init__(self, ref):
        self.ref = ref
        self.size = ref.shape[1]
        self.block = self.size // 2
        size = self.size
        self.first = [(0, 2 * size), (2 * size, 2 * size)]
        self.inner = [(4 * size, size), (5 * size, size)]
        self.twist = [(6 * size, size), (7 * size, size)]
        self.last = [[(8 * size, size), (9 * size, size)], [(10 * size, size), (11 * size, size)]]

    def rows(self, span):
        return self.ref[span[0] : span[0] + span[1], :]

    def turns(self):
        wide = self.rows(self.twist[0]).astype(F32) + self.rows(self.twist[1]).astype(F32)
        return (wide[:, : self.block], wide[:, self.block :])


def halves(wide):
    high = wide.astype(BF16)
    low = (wide - high.astype(F32)).astype(BF16)
    return (high, low)


def mul(left, right, flip=False):
    dims = (((1,), (1 if flip else 0,)), ((), ()))
    return lax.dot_general(left, right, dims, preferred_element_type=F32)


def to_values(signal, table, turn_re, turn_im):
    rows, width = signal.shape
    block = table.block
    part = mul(table.rows(table.first[0]), signal) + mul(table.rows(table.first[1]), signal)
    turned = []
    for i in range(width // block):
        part_re = part[:rows, i * block : (i + 1) * block]
        part_im = part[rows:, i * block : (i + 1) * block]
        turned.append(
            jnp.concatenate(
                [part_re * turn_re - part_im * turn_im, part_re * turn_im + part_im * turn_re],
                axis=1,
            )
        )
    high, low = halves(jnp.concatenate(turned, axis=0))
    inner = [table.rows(span) for span in table.inner]
    values = mul(high, inner[0]) + (mul(high, inner[1]) + mul(low, inner[0]))
    return [
        (values[i * rows : (i + 1) * rows, :block], values[i * rows : (i + 1) * rows, block:])
        for i in range(width // block)
    ]


def to_signal(value_re, value_im, table, turn_re, turn_im):
    block = table.block
    high, low = halves(jnp.concatenate([value_re, value_im], axis=1))
    inner = [table.rows(span) for span in table.inner]
    back = mul(high, inner[0], True) + (mul(high, inner[1], True) + mul(low, inner[0], True))
    back_re, back_im = back[:, :block], back[:, block:]
    turned = (back_re * turn_re + back_im * turn_im, back_im * turn_re - back_re * turn_im)
    out = None
    for wide, (span_high, span_low) in zip(turned, table.last):
        high, low = halves(wide)
        last = table.rows(span_high)
        term = mul(last, high) + (mul(last, low) + mul(table.rows(span_low), high))
        out = term if out is None else out + term
    return out


def call(body, name, args, outs, scratch=()):
    whole = pl.BlockSpec(memory_space=pltpu.VMEM)
    apart = pl.BlockSpec(memory_space=pltpu.HBM)
    return pl.pallas_call(
        body,
        out_shape=[
            (pltpu.VMEM if keep else pltpu.HBM)(shape, dtype)
            for shape, dtype, keep in outs
        ],
        in_specs=[whole if keep else apart for _, keep in args],
        out_specs=[whole if keep else apart for _, _, keep in outs],
        scratch_shapes=list(scratch),
        compiler_params=pltpu.CompilerParams(vmem_limit_bytes=VMEM_LIMIT),
        name=name,
    )(
        *[
            pltpu.with_memory_space_constraint(x, pltpu.VMEM if keep else pltpu.HBM)
            for x, keep in args
        ]
    )


def source_body(
    key_hbm,
    value_hbm,
    filter_hbm,
    query_hbm,
    grad_hbm,
    gain_hbm,
    table_hbm,
    packed_ref,
    key_ref,
    value_ref,
    query_ref,
    grad_ref,
    gain_ref,
    table_ref,
    filter_ref,
    sems,
):
    pairs = [
        (key_hbm, key_ref),
        (value_hbm, value_ref),
        (filter_hbm, filter_ref),
        (query_hbm, query_ref),
        (grad_hbm, grad_ref),
        (gain_hbm, gain_ref),
        (table_hbm, table_ref),
    ]
    copies = [pltpu.make_async_copy(a, b, sems.at[i]) for i, (a, b) in enumerate(pairs)]
    for copy in copies:
        copy.start()
    for copy in copies[:3]:
        copy.wait()
    peers, double, block = packed_ref.shape
    source = (key_ref[...].astype(F32) * value_ref[...].astype(F32)).astype(BF16).astype(F32)
    source = source.T.reshape(peers, double // 2, block)
    taps = filter_ref[...].astype(F32).reshape(peers, double // 2, block)
    packed_ref[...] = jnp.concatenate([source, taps], axis=1).astype(BF16)
    for copy in copies[3:]:
        copy.wait()


def convolve_body(
    packed_ref,
    query_ref,
    grad_ref,
    gain_ref,
    table_ref,
    out_ref,
    values_ref,
    query_t_ref,
    gained_t_ref,
):
    table = Table(table_ref)
    turns = table.turns()
    peers, double, block = packed_ref.shape
    per = double // 2
    packed = packed_ref[...].astype(F32)
    source = packed[:, :per].reshape(peers * per, block)
    taps = packed[:, per:].reshape(peers * per, block)
    signal = jnp.concatenate([source, taps], axis=1).astype(BF16)
    (src_re, src_im), (tap_re, tap_im) = to_values(signal, table, *turns)
    values_ref[0] = tap_re
    values_ref[1] = tap_im
    query_t_ref[...] = query_ref[...].astype(F32).T.astype(BF16)
    gained_t_ref[...] = (grad_ref[...].astype(F32) * gain_ref[...]).T
    out = to_signal(
        src_re * tap_re - src_im * tap_im, src_re * tap_im + src_im * tap_re, table, *turns
    )
    out_ref[...] = out.reshape(peers, per, block).astype(BF16)


def product_of(conv_ref, query_ref):
    peers, per, block = conv_ref.shape
    conv = conv_ref[...].astype(F32).reshape(peers * per, block)
    query = query_ref[...].astype(F32)
    return (conv, query, (query * conv).astype(BF16).astype(F32))


def partial_body(conv_ref, query_ref, gained_ref, out_ref):
    _, _, product = product_of(conv_ref, query_ref)
    square = jnp.sum(product * product, axis=0, keepdims=True)
    cross = jnp.sum(gained_ref[...] * product, axis=0, keepdims=True)
    both = jnp.concatenate([square, cross], axis=0)
    out_ref[...] = jnp.broadcast_to(both[None], out_ref.shape)


def token_scales(sums_ref, width):
    sums = jnp.sum(sums_ref[...], axis=0)
    scale = lax.rsqrt(sums[0:1] / width + EPSILON)
    return (scale, sums[1:2] * scale * scale * scale / width)


def weighted_body(
    sums_ref, conv_ref, query_ref, gained_ref, weighted_ref, grad_ref, scaled_ref, *, width
):
    scale, pull = token_scales(sums_ref, width)
    conv, query, product = product_of(conv_ref, query_ref)
    scaled = product * scale
    grad = (gained_ref[...] * scale - product * pull).astype(BF16).astype(F32)
    weighted_ref[...] = (grad * query).reshape(weighted_ref.shape).astype(BF16)
    scaled_ref[...] = scaled
    grad_ref[...] = (grad * conv).astype(BF16)


def correlate_body(
    weighted_ref,
    values_ref,
    scaled_ref,
    grad_ref,
    gain_ref,
    table_ref,
    out_ref,
    normed_hbm,
    query_grad_hbm,
    normed_ref,
    query_grad_ref,
    sems,
):
    normed_ref[...] = (scaled_ref[...].T * gain_ref[...]).astype(BF16)
    query_grad_ref[...] = grad_ref[...].astype(F32).T.astype(BF16)
    copies = [
        pltpu.make_async_copy(normed_ref, normed_hbm, sems.at[0]),
        pltpu.make_async_copy(query_grad_ref, query_grad_hbm, sems.at[1]),
    ]
    for copy in copies:
        copy.start()
    table = Table(table_ref)
    turns = table.turns()
    peers, per, block = weighted_ref.shape
    signal = weighted_ref[...].astype(F32).reshape(peers * per, block).astype(BF16)
    ((sig_re, sig_im),) = to_values(signal, table, *turns)
    tap_re, tap_im = values_ref[0], values_ref[1]
    out = to_signal(
        sig_re * tap_re + sig_im * tap_im, sig_im * tap_re - sig_re * tap_im, table, *turns
    )
    out_ref[...] = out.reshape(peers, per, block).astype(BF16)
    for copy in copies:
        copy.wait()


def finish_body(
    spread_ref, key_ref, value_ref, key_hbm, value_hbm, key_grad_ref, value_grad_ref, sems
):
    peers, per, block = spread_ref.shape
    spread = spread_ref[...].astype(F32).reshape(peers * per, block).T
    key_grad_ref[...] = (spread * value_ref[...].astype(F32)).astype(BF16)
    first = pltpu.make_async_copy(key_grad_ref, key_hbm, sems.at[0])
    first.start()
    value_grad_ref[...] = (spread * key_ref[...].astype(F32)).astype(BF16)
    second = pltpu.make_async_copy(value_grad_ref, value_hbm, sems.at[1])
    second.start()
    first.wait()
    second.wait()


def per_device(query, key, value, filters, gain, out_grad):
    peers = lax.axis_size("seq")
    groups = lax.axis_size("chan")
    block, wide = query.shape
    per = wide // peers
    width = float(wide * groups)
    table = jnp.asarray(make_table(peers, block, per))
    gain = gain.reshape(1, wide)
    home = (block, wide)
    turned = (wide, block)
    owned = (peers, per, block)

    def exchange(array, axis="seq"):
        return lax.all_to_all(array, axis, split_axis=0, concat_axis=0, tiled=True)

    def dma(count):
        return pltpu.SemaphoreType.DMA((count,))

    packed, key, value, query, out_grad, gain, table = call(
        source_body,
        "source",
        [(x, False) for x in (key, value, filters, query, out_grad, gain, table)],
        [((peers, 2 * per, block), BF16, True)]
        + [(home, BF16, True)] * 4
        + [((1, wide), F32, True), (table.shape, BF16, True)],
        [pltpu.VMEM(turned, BF16), dma(7)],
    )
    packed = exchange(packed)
    conv, values, query_t, gained_t = call(
        convolve_body,
        "convolve",
        [(x, True) for x in (packed, query, out_grad, gain, table)],
        [
            (owned, BF16, True),
            ((2, wide, block), F32, True),
            (turned, BF16, True),
            (turned, F32, True),
        ],
    )
    conv = exchange(conv)
    (partial,) = call(
        partial_body,
        "partial",
        [(x, True) for x in (conv, query_t, gained_t)],
        [((groups, 2, block), F32, True)],
    )
    sums = exchange(partial, "chan")
    weighted, grad, scaled = call(
        functools.partial(weighted_body, width=width),
        "weighted",
        [(x, True) for x in (sums, conv, query_t, gained_t)],
        [(owned, BF16, True), (turned, BF16, True), (turned, F32, True)],
    )
    weighted = exchange(weighted)
    spread, normed, query_grad = call(
        correlate_body,
        "correlate",
        [(x, True) for x in (weighted, values, scaled, grad, gain, table)],
        [(owned, BF16, True), (home, BF16, False), (home, BF16, False)],
        [pltpu.VMEM(home, BF16), pltpu.VMEM(home, BF16), dma(2)],
    )
    spread = exchange(spread)
    key_grad, value_grad = call(
        finish_body,
        "finish",
        [(x, True) for x in (spread, key, value)],
        [(home, BF16, False), (home, BF16, False)],
        [pltpu.VMEM(home, BF16), pltpu.VMEM(home, BF16), dma(2)],
    )
    return (normed, query_grad, key_grad, value_grad)


def solution(mesh):
    tokens = P("seq", "chan")
    return jax.shard_map(
        per_device,
        mesh=mesh,
        in_specs=(tokens, tokens, tokens, P("chan", "seq"), P("chan"), tokens),
        out_specs=(tokens, tokens, tokens, tokens),
        check_vma=False,
    )
```

```python
import functools

import jax
import jax.numpy as jnp
import numpy as np
from jax import lax
from jax.experimental import pallas as pl
from jax.experimental.pallas import tpu as pltpu
from jax.sharding import PartitionSpec as P

D = 8192
EPSILON = 1e-05

BF16 = jnp.bfloat16
F32 = jnp.float32

SEQ = ("y_lo", "z")
CHAN = ("x", "y_hi", "core")
LINE = ("x", "core")
PLANE = ("y_lo", "z", "y_hi")
VMEM_LIMIT = 24 << 20


def split_halves(table):
    high = table.astype(jnp.bfloat16)
    low = (table - high.astype(np.float64)).astype(jnp.bfloat16)
    return [high, low]


def make_table(blocks, block, rows):
    length = blocks * block
    steps = np.arange(blocks)
    outer = np.exp(-2j * np.pi * np.outer(steps + 0.25, steps) / blocks)
    eye = np.eye(rows)
    first = np.kron(np.concatenate([outer.real, outer.imag], axis=0), eye)
    last = [np.kron(part.T, eye) / length for part in (outer.real, outer.imag)]
    twist = np.exp(-2j * np.pi * np.outer(steps + 0.25, np.arange(block)) / length)
    twist = np.repeat(np.concatenate([twist.real, twist.imag], axis=1), rows, axis=0)
    angle = 2 * np.pi * (np.outer(np.arange(block), np.arange(block)) % block) / block
    inner = np.block([[np.cos(angle), -np.sin(angle)], [np.sin(angle), np.cos(angle)]])
    parts = split_halves(first) + split_halves(inner) + split_halves(twist)
    parts = parts + split_halves(last[0]) + split_halves(last[1])
    return np.concatenate(parts, axis=0)


class Table:
    def __init__(self, ref):
        self.ref = ref
        self.size = ref.shape[1]
        self.block = self.size // 2
        size = self.size
        self.first = [(0, 2 * size), (2 * size, 2 * size)]
        self.inner = [(4 * size, size), (5 * size, size)]
        self.twist = [(6 * size, size), (7 * size, size)]
        self.last = [[(8 * size, size), (9 * size, size)], [(10 * size, size), (11 * size, size)]]

    def rows(self, span):
        return self.ref[span[0] : span[0] + span[1], :]

    def turns(self):
        wide = self.rows(self.twist[0]).astype(F32) + self.rows(self.twist[1]).astype(F32)
        return (wide[:, : self.block], wide[:, self.block :])


def halves(wide):
    high = wide.astype(BF16)
    low = (wide - high.astype(F32)).astype(BF16)
    return (high, low)


def mul(left, right, flip=False):
    dims = (((1,), (1 if flip else 0,)), ((), ()))
    return lax.dot_general(left, right, dims, preferred_element_type=F32)


def to_values(signal, table, turn_re, turn_im):
    rows, width = signal.shape
    block = table.block
    part = mul(table.rows(table.first[0]), signal) + mul(table.rows(table.first[1]), signal)
    turned = []
    for i in range(width // block):
        part_re = part[:rows, i * block : (i + 1) * block]
        part_im = part[rows:, i * block : (i + 1) * block]
        turned.append(
            jnp.concatenate(
                [part_re * turn_re - part_im * turn_im, part_re * turn_im + part_im * turn_re],
                axis=1,
            )
        )
    high, low = halves(jnp.concatenate(turned, axis=0))
    inner = [table.rows(span) for span in table.inner]
    values = mul(high, inner[0]) + (mul(high, inner[1]) + mul(low, inner[0]))
    return [
        (values[i * rows : (i + 1) * rows, :block], values[i * rows : (i + 1) * rows, block:])
        for i in range(width // block)
    ]


def to_signal(value_re, value_im, table, turn_re, turn_im):
    block = table.block
    high, low = halves(jnp.concatenate([value_re, value_im], axis=1))
    inner = [table.rows(span) for span in table.inner]
    back = mul(high, inner[0], True) + (mul(high, inner[1], True) + mul(low, inner[0], True))
    back_re, back_im = back[:, :block], back[:, block:]
    turned = (back_re * turn_re + back_im * turn_im, back_im * turn_re - back_re * turn_im)
    out = None
    for wide, (span_high, span_low) in zip(turned, table.last):
        high, low = halves(wide)
        last = table.rows(span_high)
        term = mul(last, high) + (mul(last, low) + mul(table.rows(span_low), high))
        out = term if out is None else out + term
    return out


def call(body, name, args, outs, scratch=()):
    whole = pl.BlockSpec(memory_space=pltpu.VMEM)
    apart = pl.BlockSpec(memory_space=pltpu.HBM)
    return pl.pallas_call(
        body,
        out_shape=[
            (pltpu.VMEM if keep else pltpu.HBM)(shape, dtype)
            for shape, dtype, keep in outs
        ],
        in_specs=[whole if keep else apart for _, keep in args],
        out_specs=[whole if keep else apart for _, _, keep in outs],
        scratch_shapes=list(scratch),
        compiler_params=pltpu.CompilerParams(vmem_limit_bytes=VMEM_LIMIT),
        name=name,
    )(
        *[
            pltpu.with_memory_space_constraint(x, pltpu.VMEM if keep else pltpu.HBM)
            for x, keep in args
        ]
    )


def source_body(
    key_hbm,
    value_hbm,
    filter_hbm,
    query_hbm,
    grad_hbm,
    gain_hbm,
    table_hbm,
    packed_ref,
    key_ref,
    value_ref,
    query_ref,
    grad_ref,
    gain_ref,
    table_ref,
    filter_ref,
    sems,
):
    pairs = [
        (query_hbm, query_ref),
        (grad_hbm, grad_ref),
        (key_hbm, key_ref),
        (value_hbm, value_ref),
        (filter_hbm, filter_ref),
        (gain_hbm, gain_ref),
        (table_hbm, table_ref),
    ]
    copies = [pltpu.make_async_copy(a, b, sems.at[i]) for i, (a, b) in enumerate(pairs)]
    for copy in copies:
        copy.start()
    peers, rows, block = packed_ref.shape
    per = rows // 4

    def piece(wide):
        return wide.reshape(peers, per, block)

    for copy in copies[:2]:
        copy.wait()
    query = piece(query_ref[...].astype(F32).T)
    grad = piece(grad_ref[...].astype(F32).T)
    packed_ref[:, 2 * per :, :] = jnp.concatenate([query, grad], axis=1).astype(BF16)
    for copy in copies[2:5]:
        copy.wait()
    source = (key_ref[...].astype(F32) * value_ref[...].astype(F32)).astype(BF16).astype(F32)
    taps = piece(filter_ref[...].astype(F32))
    packed_ref[:, : 2 * per, :] = jnp.concatenate([piece(source.T), taps], axis=1).astype(BF16)
    for copy in copies[5:]:
        copy.wait()


def convolve_body(packed_ref, gain_ref, table_ref, out_ref, values_ref, gained_ref, sums_ref):
    table = Table(table_ref)
    turns = table.turns()
    peers, rows, block = packed_ref.shape
    per = rows // 4
    packed = packed_ref[:, : 2 * per, :].astype(F32)
    source = packed[:, :per].reshape(peers * per, block)
    taps = packed[:, per:].reshape(peers * per, block)
    signal = jnp.concatenate([source, taps], axis=1).astype(BF16)
    (src_re, src_im), (tap_re, tap_im) = to_values(signal, table, *turns)
    values_ref[0] = tap_re
    values_ref[1] = tap_im
    others = packed_ref[:, 2 * per :, :].astype(F32)
    query, grad = others[:, :per], others[:, per:]
    wide = gain_ref.shape[1]
    lane = lax.broadcasted_iota(jnp.int32, (per, wide), 1)
    channel = lax.broadcasted_iota(jnp.int32, (per, wide), 0) + per * lax.axis_index(SEQ)
    picked = jnp.where(lane == channel, jnp.broadcast_to(gain_ref[...], (per, wide)), 0.0)
    gained = grad * jnp.sum(picked, axis=1, keepdims=True)[None]
    gained_ref[...] = gained
    out = to_signal(
        src_re * tap_re - src_im * tap_im, src_re * tap_im + src_im * tap_re, table, *turns
    )
    conv = out.reshape(peers, per, block).astype(BF16)
    out_ref[...] = conv
    product = (query * conv.astype(F32)).astype(BF16).astype(F32)
    square = jnp.sum(product * product, axis=1, keepdims=True)
    cross = jnp.sum(gained * product, axis=1, keepdims=True)
    half = peers // 2
    sums_ref[...] = jnp.concatenate(
        [square[:half], square[half:], cross[:half], cross[half:]], axis=1
    )


def merge_body(sums_ref, out_ref):
    total = jnp.sum(sums_ref[...].astype(F32), axis=0, keepdims=True)
    out_ref[...] = jnp.broadcast_to(total, out_ref.shape).astype(out_ref.dtype)


def scales_of(square, cross, width):
    scale = lax.rsqrt(square / width + EPSILON)
    return (scale, cross * scale * scale * scale / width)


def correlate_body(
    sums_ref, packed_ref, conv_ref, gained_ref, values_ref, table_ref, out_ref, *, width
):
    table = Table(table_ref)
    turns = table.turns()
    peers, per, block = conv_ref.shape
    square = jnp.concatenate([sums_ref[:, 0:1, :], sums_ref[:, 1:2, :]], axis=0)
    cross = jnp.concatenate([sums_ref[:, 2:3, :], sums_ref[:, 3:4, :]], axis=0)
    scale, pull = scales_of(square, cross, width)
    conv = conv_ref[...].astype(F32)
    query = packed_ref[:, 2 * per :, :].astype(F32)[:, :per]
    product = (query * conv).astype(BF16).astype(F32)
    grad = (gained_ref[...] * scale - product * pull).astype(BF16).astype(F32)
    signal = (grad * query).reshape(peers * per, block).astype(BF16)
    ((sig_re, sig_im),) = to_values(signal, table, *turns)
    tap_re, tap_im = values_ref[0], values_ref[1]
    out = to_signal(
        sig_re * tap_re + sig_im * tap_im, sig_im * tap_re - sig_re * tap_im, table, *turns
    )
    spread = out.reshape(peers, per, block)
    out_ref[...] = jnp.concatenate([conv, spread], axis=1).astype(BF16)


def finish_body(
    back_ref,
    sums_ref,
    key_ref,
    value_ref,
    query_ref,
    grad_ref,
    gain_ref,
    normed_hbm,
    query_grad_hbm,
    key_grad_hbm,
    value_grad_hbm,
    outs_ref,
    sems,
    *,
    width,
):
    peers, rows, block = back_ref.shape
    per = rows // 2
    outs = [normed_hbm, query_grad_hbm, key_grad_hbm, value_grad_hbm]
    copies = [pltpu.make_async_copy(outs_ref.at[i], out, sems.at[i]) for i, out in enumerate(outs)]

    def put(i, wide):
        outs_ref[i] = wide.astype(BF16)
        copies[i].start()

    back = back_ref[...].astype(F32)
    spread = back[:, per:].reshape(peers * per, block).T
    put(2, spread * value_ref[...].astype(F32))
    put(3, spread * key_ref[...].astype(F32))
    half = peers // 2
    place = lax.axis_index(SEQ)
    mine = sums_ref[place % half]
    upper = place >= half
    square = jnp.where(upper, mine[1:2], mine[0:1])
    cross = jnp.where(upper, mine[3:4], mine[2:3])
    scale, pull = scales_of(square, cross, width)
    tall = (block, block)
    scale = jnp.broadcast_to(scale, tall).T[:, 0:1]
    pull = jnp.broadcast_to(pull, tall).T[:, 0:1]
    conv = back[:, :per].reshape(peers * per, block).T
    gain = gain_ref[...]
    product = (query_ref[...].astype(F32) * conv).astype(BF16).astype(F32)
    put(0, product * scale * gain)
    gained = grad_ref[...].astype(F32) * gain
    grad = (gained * scale - product * pull).astype(BF16).astype(F32)
    put(1, grad * conv)
    for copy in copies:
        copy.wait()


def per_device(query, key, value, filters, gain, out_grad):
    peers = lax.axis_size(SEQ)
    groups = lax.axis_size(CHAN)
    line = lax.axis_size(LINE)
    plane = lax.axis_size(PLANE)
    block, wide = query.shape
    per = wide // peers
    width = float(wide * groups)
    table = jnp.asarray(make_table(peers, block, per))
    gain = gain.reshape(1, wide)
    home = (block, wide)
    owned = (peers, per, block)
    chunk = 2 * peers // line

    def exchange(array, axes):
        return lax.all_to_all(array, axes, split_axis=0, concat_axis=0, tiled=True)

    def merge(array, count, dtype, name):
        return call(
            merge_body, name, [(array, True)], [((count, chunk, block), dtype, True)]
        )[0]

    def dma(count):
        return pltpu.SemaphoreType.DMA((count,))

    packed, key, value, query, out_grad, gain, table = call(
        source_body,
        "source",
        [(x, False) for x in (key, value, filters, query, out_grad, gain, table)],
        [((peers, 4 * per, block), BF16, True)]
        + [(home, BF16, True)] * 4
        + [((1, wide), F32, True), (table.shape, BF16, True)],
        [pltpu.VMEM((wide, block), BF16), dma(7)],
    )
    packed = exchange(packed, SEQ)
    conv, values, gained, sums = call(
        convolve_body,
        "convolve",
        [(x, True) for x in (packed, gain, table)],
        [
            (owned, BF16, True),
            ((2, wide, block), F32, True),
            (owned, F32, True),
            ((line, chunk, block), F32, True),
        ],
    )
    sums = exchange(sums, LINE)
    sums = exchange(merge(sums, plane, F32, "merge_line"), PLANE)
    sums = exchange(merge(sums, line, F32, "merge_plane"), LINE)
    (back,) = call(
        functools.partial(correlate_body, width=width),
        "correlate",
        [(x, True) for x in (sums, packed, conv, gained, values, table)],
        [((peers, 2 * per, block), BF16, True)],
    )
    back = exchange(back, SEQ)
    return tuple(
        call(
            functools.partial(finish_body, width=width),
            "finish",
            [(x, True) for x in (back, sums, key, value, query, out_grad, gain)],
            [(home, BF16, False)] * 4,
            [pltpu.VMEM((4,) + home, BF16), dma(4)],
        )
    )


def solution(mesh):
    cut = jax.sharding.Mesh(mesh.devices.reshape(4, 8, 8, 2, 2), SEQ + CHAN)
    tokens = P(SEQ, CHAN)
    return jax.shard_map(
        per_device,
        mesh=cut,
        in_specs=(tokens, tokens, tokens, P(CHAN, SEQ), P(CHAN), tokens),
        out_specs=(tokens, tokens, tokens, tokens),
        check_vma=False,
    )
```

```python
import functools

import jax
import jax.numpy as jnp
import numpy as np
from jax import lax
from jax.experimental import pallas as pl
from jax.experimental.pallas import tpu as pltpu
from jax.sharding import PartitionSpec as P

D = 8192
EPSILON = 1e-05

BF16 = jnp.bfloat16
F32 = jnp.float32

SEQ = ("y_lo", "z")
CHAN = ("x", "y_hi", "core")
LINE = ("x", "core")
PLANE = ("y_lo", "z", "y_hi")
VMEM_LIMIT = 24 << 20


def split_halves(table):
    high = table.astype(jnp.bfloat16)
    low = (table - high.astype(np.float64)).astype(jnp.bfloat16)
    return [high, low]


def make_tables(blocks, block, rows):
    length = blocks * block
    steps = np.arange(blocks)
    outer = np.exp(-2j * np.pi * np.outer(steps + 0.25, steps) / blocks)
    eye = np.eye(rows)
    first = np.kron(np.concatenate([outer.real, outer.imag], axis=0), eye)
    last = [np.kron(part.T, eye) / length for part in (outer.real, outer.imag)]
    twist = np.exp(-2j * np.pi * np.outer(steps + 0.25, np.arange(block)) / length)
    twist = np.concatenate([twist.real, twist.imag], axis=1).astype(np.float32)
    angle = 2 * np.pi * (np.outer(np.arange(block), np.arange(block)) % block) / block
    inner = np.block([[np.cos(angle), -np.sin(angle)], [np.sin(angle), np.cos(angle)]])
    parts = split_halves(first) + split_halves(inner)
    parts = parts + split_halves(last[0]) + split_halves(last[1])
    return (np.concatenate(parts, axis=0), twist)


class Table:
    def __init__(self, ref, twist_ref):
        self.ref = ref
        self.size = size = ref.shape[1]
        self.block = size // 2
        self.first = [(0, 2 * size), (2 * size, 2 * size)]
        self.inner = [(4 * size, size), (5 * size, size)]
        self.last = [[(6 * size, size), (7 * size, size)], [(8 * size, size), (9 * size, size)]]
        peers = twist_ref.shape[0]
        tall = (peers, size // peers, size)
        twist = jnp.broadcast_to(twist_ref[...].reshape(peers, 1, size), tall).reshape(size, size)
        self.turns = (twist[:, : self.block], twist[:, self.block :])

    def rows(self, span):
        return self.ref[span[0] : span[0] + span[1], :]


def halves(wide):
    high = wide.astype(BF16)
    low = (wide - high.astype(F32)).astype(BF16)
    return (high, low)


def mul(left, right, flip=False):
    dims = (((1,), (1 if flip else 0,)), ((), ()))
    return lax.dot_general(left, right, dims, preferred_element_type=F32)


def to_values(signal, table, turn_re, turn_im):
    rows, width = signal.shape
    block = table.block
    part = mul(table.rows(table.first[0]), signal) + mul(table.rows(table.first[1]), signal)
    turned = []
    for i in range(width // block):
        part_re = part[:rows, i * block : (i + 1) * block]
        part_im = part[rows:, i * block : (i + 1) * block]
        turned.append(
            jnp.concatenate(
                [part_re * turn_re - part_im * turn_im, part_re * turn_im + part_im * turn_re],
                axis=1,
            )
        )
    high, low = halves(jnp.concatenate(turned, axis=0))
    inner = [table.rows(span) for span in table.inner]
    values = mul(high, inner[0]) + (mul(high, inner[1]) + mul(low, inner[0]))
    return [
        (values[i * rows : (i + 1) * rows, :block], values[i * rows : (i + 1) * rows, block:])
        for i in range(width // block)
    ]


def to_signal(value_re, value_im, table, turn_re, turn_im):
    block = table.block
    high, low = halves(jnp.concatenate([value_re, value_im], axis=1))
    inner = [table.rows(span) for span in table.inner]
    back = mul(high, inner[0], True) + (mul(high, inner[1], True) + mul(low, inner[0], True))
    back_re, back_im = back[:, :block], back[:, block:]
    turned = (back_re * turn_re + back_im * turn_im, back_im * turn_re - back_re * turn_im)
    out = None
    for wide, (span_high, span_low) in zip(turned, table.last):
        high, low = halves(wide)
        both = mul(table.rows(span_high), jnp.concatenate([high, low], axis=1))
        term = both[:, :block] + (both[:, block:] + mul(table.rows(span_low), high))
        out = term if out is None else out + term
    return out


def call(body, name, args, outs, scratch=()):
    whole = pl.BlockSpec(memory_space=pltpu.VMEM)
    apart = pl.BlockSpec(memory_space=pltpu.HBM)
    return pl.pallas_call(
        body,
        out_shape=[
            (pltpu.VMEM if keep else pltpu.HBM)(shape, dtype)
            for shape, dtype, keep in outs
        ],
        in_specs=[whole if keep else apart for _, keep in args],
        out_specs=[whole if keep else apart for _, _, keep in outs],
        scratch_shapes=list(scratch),
        compiler_params=pltpu.CompilerParams(vmem_limit_bytes=VMEM_LIMIT),
        name=name,
    )(
        *[
            pltpu.with_memory_space_constraint(x, pltpu.VMEM if keep else pltpu.HBM)
            for x, keep in args
        ]
    )


def source_body(
    key_hbm,
    value_hbm,
    filter_hbm,
    query_hbm,
    grad_hbm,
    gain_hbm,
    table_hbm,
    twist_hbm,
    packed_ref,
    key_ref,
    value_ref,
    query_ref,
    grad_ref,
    gain_ref,
    table_ref,
    twist_ref,
    filter_ref,
    sems,
):
    pairs = [
        (query_hbm, query_ref),
        (grad_hbm, grad_ref),
        (key_hbm, key_ref),
        (value_hbm, value_ref),
        (filter_hbm, filter_ref),
        (gain_hbm, gain_ref),
        (twist_hbm, twist_ref),
        (table_hbm, table_ref),
    ]
    copies = [pltpu.make_async_copy(a, b, sems.at[i]) for i, (a, b) in enumerate(pairs)]
    copies[-1].start()
    for copy in copies[:-1]:
        copy.start()
    peers, rows, block = packed_ref.shape
    per = rows // 4

    def piece(wide):
        return wide.reshape(peers, per, block)

    for copy in copies[:2]:
        copy.wait()
    query = piece(query_ref[...].astype(F32).T)
    grad = piece(grad_ref[...].astype(F32).T)
    packed_ref[:, 2 * per :, :] = jnp.concatenate([query, grad], axis=1).astype(BF16)
    for copy in copies[2:5]:
        copy.wait()
    source = (key_ref[...].astype(F32) * value_ref[...].astype(F32)).astype(BF16).astype(F32)
    taps = piece(filter_ref[...].astype(F32))
    packed_ref[:, : 2 * per, :] = jnp.concatenate([piece(source.T), taps], axis=1).astype(BF16)
    for copy in copies[5:]:
        copy.wait()


def convolve_body(
    packed_ref, gain_ref, table_ref, twist_ref, out_ref, values_ref, gained_ref, sums_ref
):
    table = Table(table_ref, twist_ref)
    turns = table.turns
    peers, rows, block = packed_ref.shape
    per = rows // 4
    packed = packed_ref[:, : 2 * per, :].astype(F32)
    source = packed[:, :per].reshape(peers * per, block)
    taps = packed[:, per:].reshape(peers * per, block)
    signal = jnp.concatenate([source, taps], axis=1).astype(BF16)
    (src_re, src_im), (tap_re, tap_im) = to_values(signal, table, *turns)
    values_ref[0] = tap_re
    values_ref[1] = tap_im
    others = packed_ref[:, 2 * per :, :].astype(F32)
    query, grad = others[:, :per], others[:, per:]
    wide = gain_ref.shape[1]
    lane = lax.broadcasted_iota(jnp.int32, (per, wide), 1)
    channel = lax.broadcasted_iota(jnp.int32, (per, wide), 0) + per * lax.axis_index(SEQ)
    picked = jnp.where(lane == channel, jnp.broadcast_to(gain_ref[...], (per, wide)), 0.0)
    gained = grad * jnp.sum(picked, axis=1, keepdims=True)[None]
    gained_ref[...] = gained
    out = to_signal(
        src_re * tap_re - src_im * tap_im, src_re * tap_im + src_im * tap_re, table, *turns
    )
    conv = out.reshape(peers, per, block).astype(BF16)
    out_ref[...] = conv
    product = (query * conv.astype(F32)).astype(BF16).astype(F32)
    square = jnp.sum(product * product, axis=1, keepdims=True)
    cross = jnp.sum(gained * product, axis=1, keepdims=True)
    half = peers // 2
    sums_ref[...] = jnp.concatenate(
        [square[:half], square[half:], cross[:half], cross[half:]], axis=1
    )


def merge_body(sums_ref, out_ref):
    total = jnp.sum(sums_ref[...].astype(F32), axis=0, keepdims=True)
    out_ref[...] = jnp.broadcast_to(total, out_ref.shape).astype(out_ref.dtype)


def scales_of(square, cross, width):
    scale = lax.rsqrt(square / width + EPSILON)
    return (scale, cross * scale * scale * scale / width)


def correlate_body(
    sums_ref,
    packed_ref,
    conv_ref,
    gained_ref,
    values_ref,
    table_ref,
    twist_ref,
    out_ref,
    *,
    width,
):
    table = Table(table_ref, twist_ref)
    turns = table.turns
    peers, per, block = conv_ref.shape
    square = jnp.concatenate([sums_ref[:, 0:1, :], sums_ref[:, 1:2, :]], axis=0)
    cross = jnp.concatenate([sums_ref[:, 2:3, :], sums_ref[:, 3:4, :]], axis=0)
    scale, pull = scales_of(square, cross, width)
    conv = conv_ref[...].astype(F32)
    query = packed_ref[:, 2 * per :, :].astype(F32)[:, :per]
    product = (query * conv).astype(BF16).astype(F32)
    grad = (gained_ref[...] * scale - product * pull).astype(BF16).astype(F32)
    signal = (grad * query).reshape(peers * per, block).astype(BF16)
    ((sig_re, sig_im),) = to_values(signal, table, *turns)
    tap_re, tap_im = values_ref[0], values_ref[1]
    out = to_signal(
        sig_re * tap_re + sig_im * tap_im, sig_im * tap_re - sig_re * tap_im, table, *turns
    )
    spread = out.reshape(peers, per, block)
    out_ref[...] = jnp.concatenate([conv, spread], axis=1).astype(BF16)


def finish_body(
    back_ref,
    sums_ref,
    key_ref,
    value_ref,
    query_ref,
    grad_ref,
    gain_ref,
    normed_hbm,
    query_grad_hbm,
    key_grad_hbm,
    value_grad_hbm,
    outs_ref,
    sems,
    *,
    width,
):
    peers, rows, block = back_ref.shape
    per = rows // 2
    outs = [normed_hbm, query_grad_hbm, key_grad_hbm, value_grad_hbm]
    copies = [pltpu.make_async_copy(outs_ref.at[i], out, sems.at[i]) for i, out in enumerate(outs)]

    def put(i, wide):
        outs_ref[i] = wide.astype(BF16)
        copies[i].start()

    back = back_ref[...].astype(F32)
    spread = back[:, per:].reshape(peers * per, block).T
    put(2, spread * value_ref[...].astype(F32))
    put(3, spread * key_ref[...].astype(F32))
    half = peers // 2
    place = lax.axis_index(SEQ)
    mine = sums_ref[place % half]
    upper = place >= half
    square = jnp.where(upper, mine[1:2], mine[0:1])
    cross = jnp.where(upper, mine[3:4], mine[2:3])
    scale, pull = scales_of(square, cross, width)
    tall = (block, block)
    scale = jnp.broadcast_to(scale, tall).T[:, 0:1]
    pull = jnp.broadcast_to(pull, tall).T[:, 0:1]
    conv = back[:, :per].reshape(peers * per, block).T
    gain = gain_ref[...]
    product = (query_ref[...].astype(F32) * conv).astype(BF16).astype(F32)
    put(0, product * scale * gain)
    gained = grad_ref[...].astype(F32) * gain
    grad = (gained * scale - product * pull).astype(BF16).astype(F32)
    put(1, grad * conv)
    for copy in copies:
        copy.wait()


def per_device(query, key, value, filters, gain, out_grad):
    peers = lax.axis_size(SEQ)
    groups = lax.axis_size(CHAN)
    line = lax.axis_size(LINE)
    plane = lax.axis_size(PLANE)
    block, wide = query.shape
    per = wide // peers
    width = float(wide * groups)
    table, twist = (jnp.asarray(part) for part in make_tables(peers, block, per))
    gain = gain.reshape(1, wide)
    home = (block, wide)
    owned = (peers, per, block)
    chunk = 2 * peers // line

    def exchange(array, axes):
        return lax.all_to_all(array, axes, split_axis=0, concat_axis=0, tiled=True)

    def merge(array, count, dtype, name):
        return call(
            merge_body, name, [(array, True)], [((count, chunk, block), dtype, True)]
        )[0]

    def dma(count):
        return pltpu.SemaphoreType.DMA((count,))

    packed, key, value, query, out_grad, gain, table, twist = call(
        source_body,
        "source",
        [(x, False) for x in (key, value, filters, query, out_grad, gain, table, twist)],
        [((peers, 4 * per, block), BF16, True)]
        + [(home, BF16, True)] * 4
        + [((1, wide), F32, True), (table.shape, BF16, True), (twist.shape, F32, True)],
        [pltpu.VMEM((wide, block), BF16), dma(8)],
    )
    packed = exchange(packed, SEQ)
    conv, values, gained, sums = call(
        convolve_body,
        "convolve",
        [(x, True) for x in (packed, gain, table, twist)],
        [
            (owned, BF16, True),
            ((2, wide, block), F32, True),
            (owned, F32, True),
            ((line, chunk, block), F32, True),
        ],
    )
    sums = exchange(sums, LINE)
    sums = exchange(merge(sums, plane, BF16, "merge_line"), PLANE)
    sums = exchange(merge(sums, line, F32, "merge_plane"), LINE)
    (back,) = call(
        functools.partial(correlate_body, width=width),
        "correlate",
        [(x, True) for x in (sums, packed, conv, gained, values, table, twist)],
        [((peers, 2 * per, block), BF16, True)],
    )
    back = exchange(back, SEQ)
    return tuple(
        call(
            functools.partial(finish_body, width=width),
            "finish",
            [(x, True) for x in (back, sums, key, value, query, out_grad, gain)],
            [(home, BF16, False)] * 4,
            [pltpu.VMEM((4,) + home, BF16), dma(4)],
        )
    )


def solution(mesh):
    cut = jax.sharding.Mesh(mesh.devices.reshape(4, 8, 8, 2, 2), SEQ + CHAN)
    tokens = P(SEQ, CHAN)
    return jax.shard_map(
        per_device,
        mesh=cut,
        in_specs=(tokens, tokens, tokens, P(CHAN, SEQ), P(CHAN), tokens),
        out_specs=(tokens, tokens, tokens, tokens),
        check_vma=False,
    )
```

```python
import functools

import jax
import jax.numpy as jnp
import numpy as np
from jax import lax
from jax.experimental import pallas as pl
from jax.experimental.pallas import tpu as pltpu
from jax.sharding import PartitionSpec as P

D = 8192
EPSILON = 1e-05

BF16 = jnp.bfloat16
F32 = jnp.float32

SEQ = ("y_lo", "z")
CHAN = ("x", "y_hi", "core")
LINE = ("x", "core")
PLANE = ("y_lo", "z", "y_hi")
VMEM_LIMIT = 24 << 20


def split_halves(table):
    high = table.astype(jnp.bfloat16)
    low = (table - high.astype(np.float64)).astype(jnp.bfloat16)
    return [high, low]


def make_tables(blocks, block, rows):
    length = blocks * block
    steps = np.arange(blocks)
    outer = np.exp(-2j * np.pi * np.outer(steps + 0.25, steps) / blocks)
    eye = np.eye(rows)
    first = np.kron(np.concatenate([outer.real, outer.imag], axis=0), eye)
    last = [np.kron(part.T, eye) / length for part in (outer.real, outer.imag)]
    twist = np.exp(-2j * np.pi * np.outer(steps + 0.25, np.arange(block)) / length)
    twist = np.concatenate([twist.real, twist.imag], axis=1).astype(np.float32)
    angle = 2 * np.pi * (np.outer(np.arange(block), np.arange(block)) % block) / block
    inner = np.block([[np.cos(angle), -np.sin(angle)], [np.sin(angle), np.cos(angle)]])
    parts = split_halves(first) + split_halves(inner)
    parts = parts + split_halves(last[0]) + split_halves(last[1])
    return (np.concatenate(parts, axis=0), twist)


class Table:
    def __init__(self, ref, twist_ref):
        self.ref = ref
        self.size = size = ref.shape[1]
        self.block = size // 2
        self.first = [(0, 2 * size), (2 * size, 2 * size)]
        self.inner = [(4 * size, size), (5 * size, size)]
        self.last = [[(6 * size, size), (7 * size, size)], [(8 * size, size), (9 * size, size)]]
        peers = twist_ref.shape[0]
        tall = (peers, size // peers, size)
        twist = jnp.broadcast_to(twist_ref[...].reshape(peers, 1, size), tall).reshape(size, size)
        self.turns = (twist[:, : self.block], twist[:, self.block :])

    def rows(self, span):
        return self.ref[span[0] : span[0] + span[1], :]


def halves(wide):
    high = wide.astype(BF16)
    low = (wide - high.astype(F32)).astype(BF16)
    return (high, low)


def mul(left, right, flip=False):
    dims = (((1,), (1 if flip else 0,)), ((), ()))
    return lax.dot_general(left, right, dims, preferred_element_type=F32)


def to_values(signal, table, turn_re, turn_im):
    rows, width = signal.shape
    block = table.block
    part = mul(table.rows(table.first[0]), signal) + mul(table.rows(table.first[1]), signal)
    turned = []
    for i in range(width // block):
        part_re = part[:rows, i * block : (i + 1) * block]
        part_im = part[rows:, i * block : (i + 1) * block]
        turned.append(
            jnp.concatenate(
                [part_re * turn_re - part_im * turn_im, part_re * turn_im + part_im * turn_re],
                axis=1,
            )
        )
    high, low = halves(jnp.concatenate(turned, axis=0))
    inner = [table.rows(span) for span in table.inner]
    values = mul(high, inner[0]) + (mul(high, inner[1]) + mul(low, inner[0]))
    return [
        (values[i * rows : (i + 1) * rows, :block], values[i * rows : (i + 1) * rows, block:])
        for i in range(width // block)
    ]


def to_signal(value_re, value_im, table, turn_re, turn_im):
    block = table.block
    high, low = halves(jnp.concatenate([value_re, value_im], axis=1))
    inner = [table.rows(span) for span in table.inner]
    back = mul(high, inner[0], True) + (mul(high, inner[1], True) + mul(low, inner[0], True))
    back_re, back_im = back[:, :block], back[:, block:]
    turned = (back_re * turn_re + back_im * turn_im, back_im * turn_re - back_re * turn_im)
    out = None
    for wide, (span_high, span_low) in zip(turned, table.last):
        high, low = halves(wide)
        both = mul(table.rows(span_high), jnp.concatenate([high, low], axis=1))
        term = both[:, :block] + (both[:, block:] + mul(table.rows(span_low), high))
        out = term if out is None else out + term
    return out


def call(body, name, args, outs, scratch=(), cost=None):
    whole = pl.BlockSpec(memory_space=pltpu.VMEM)
    apart = pl.BlockSpec(memory_space=pltpu.HBM)
    return pl.pallas_call(
        body,
        out_shape=[
            (pltpu.VMEM if keep else pltpu.HBM)(shape, dtype)
            for shape, dtype, keep in outs
        ],
        in_specs=[whole if keep else apart for _, keep in args],
        out_specs=[whole if keep else apart for _, _, keep in outs],
        scratch_shapes=list(scratch),
        cost_estimate=cost,
        compiler_params=pltpu.CompilerParams(vmem_limit_bytes=VMEM_LIMIT),
        name=name,
    )(
        *[
            pltpu.with_memory_space_constraint(x, pltpu.VMEM if keep else pltpu.HBM)
            for x, keep in args
        ]
    )


def load_body(*refs):
    count = len(refs) // 2
    sems = refs[-1]
    copies = [
        pltpu.make_async_copy(refs[i], refs[count + i], sems.at[i]) for i in range(count)
    ]
    for copy in copies:
        copy.start()
    for copy in copies:
        copy.wait()


def pack_body(key_ref, value_ref, filter_ref, query_ref, grad_ref, packed_ref):
    peers, rows, block = packed_ref.shape
    per = rows // 4

    def piece(wide):
        return wide.reshape(peers, per, block)

    query = piece(query_ref[...].astype(F32).T)
    grad = piece(grad_ref[...].astype(F32).T)
    packed_ref[:, 2 * per :, :] = jnp.concatenate([query, grad], axis=1).astype(BF16)
    source = (key_ref[...].astype(F32) * value_ref[...].astype(F32)).astype(BF16).astype(F32)
    taps = piece(filter_ref[...].astype(F32))
    packed_ref[:, : 2 * per, :] = jnp.concatenate([piece(source.T), taps], axis=1).astype(BF16)


def convolve_body(
    packed_ref, gain_ref, table_ref, twist_ref, out_ref, values_ref, gained_ref, sums_ref
):
    table = Table(table_ref, twist_ref)
    turns = table.turns
    peers, rows, block = packed_ref.shape
    per = rows // 4
    packed = packed_ref[:, : 2 * per, :].astype(F32)
    source = packed[:, :per].reshape(peers * per, block)
    taps = packed[:, per:].reshape(peers * per, block)
    signal = jnp.concatenate([source, taps], axis=1).astype(BF16)
    (src_re, src_im), (tap_re, tap_im) = to_values(signal, table, *turns)
    values_ref[0] = tap_re
    values_ref[1] = tap_im
    others = packed_ref[:, 2 * per :, :].astype(F32)
    query, grad = others[:, :per], others[:, per:]
    wide = gain_ref.shape[1]
    lane = lax.broadcasted_iota(jnp.int32, (per, wide), 1)
    channel = lax.broadcasted_iota(jnp.int32, (per, wide), 0) + per * lax.axis_index(SEQ)
    picked = jnp.where(lane == channel, jnp.broadcast_to(gain_ref[...], (per, wide)), 0.0)
    gained = grad * jnp.sum(picked, axis=1, keepdims=True)[None]
    gained_ref[...] = gained
    out = to_signal(
        src_re * tap_re - src_im * tap_im, src_re * tap_im + src_im * tap_re, table, *turns
    )
    conv = out.reshape(peers, per, block).astype(BF16)
    out_ref[...] = conv
    product = (query * conv.astype(F32)).astype(BF16).astype(F32)
    square = jnp.sum(product * product, axis=1, keepdims=True)
    cross = jnp.sum(gained * product, axis=1, keepdims=True)
    half = peers // 2
    sums_ref[...] = jnp.concatenate(
        [square[:half], square[half:], cross[:half], cross[half:]], axis=1
    )


def merge_body(sums_ref, out_ref):
    total = jnp.sum(sums_ref[...].astype(F32), axis=0, keepdims=True)
    out_ref[...] = jnp.broadcast_to(total, out_ref.shape).astype(out_ref.dtype)


def scales_of(square, cross, width):
    scale = lax.rsqrt(square / width + EPSILON)
    return (scale, cross * scale * scale * scale / width)


def correlate_body(
    sums_ref,
    packed_ref,
    conv_ref,
    gained_ref,
    values_ref,
    table_ref,
    twist_ref,
    out_ref,
    *,
    width,
):
    table = Table(table_ref, twist_ref)
    turns = table.turns
    peers, per, block = conv_ref.shape
    square = jnp.concatenate([sums_ref[:, 0:1, :], sums_ref[:, 1:2, :]], axis=0)
    cross = jnp.concatenate([sums_ref[:, 2:3, :], sums_ref[:, 3:4, :]], axis=0)
    scale, pull = scales_of(square, cross, width)
    conv = conv_ref[...].astype(F32)
    query = packed_ref[:, 2 * per :, :].astype(F32)[:, :per]
    product = (query * conv).astype(BF16).astype(F32)
    grad = (gained_ref[...] * scale - product * pull).astype(BF16).astype(F32)
    signal = (grad * query).reshape(peers * per, block).astype(BF16)
    ((sig_re, sig_im),) = to_values(signal, table, *turns)
    tap_re, tap_im = values_ref[0], values_ref[1]
    out = to_signal(
        sig_re * tap_re + sig_im * tap_im, sig_im * tap_re - sig_re * tap_im, table, *turns
    )
    spread = out.reshape(peers, per, block)
    out_ref[...] = jnp.concatenate([conv, spread], axis=1).astype(BF16)


def finish_body(
    back_ref,
    sums_ref,
    key_ref,
    value_ref,
    query_ref,
    grad_ref,
    gain_ref,
    normed_hbm,
    query_grad_hbm,
    key_grad_hbm,
    value_grad_hbm,
    outs_ref,
    sems,
    *,
    width,
):
    peers, rows, block = back_ref.shape
    per = rows // 2
    outs = [normed_hbm, query_grad_hbm, key_grad_hbm, value_grad_hbm]
    copies = [pltpu.make_async_copy(outs_ref.at[i], out, sems.at[i]) for i, out in enumerate(outs)]

    def put(i, wide):
        outs_ref[i] = wide.astype(BF16)
        copies[i].start()

    back = back_ref[...].astype(F32)
    spread = back[:, per:].reshape(peers * per, block).T
    put(2, spread * value_ref[...].astype(F32))
    put(3, spread * key_ref[...].astype(F32))
    half = peers // 2
    place = lax.axis_index(SEQ)
    mine = sums_ref[place % half]
    upper = place >= half
    square = jnp.where(upper, mine[1:2], mine[0:1])
    cross = jnp.where(upper, mine[3:4], mine[2:3])
    scale, pull = scales_of(square, cross, width)
    tall = (block, block)
    scale = jnp.broadcast_to(scale, tall).T[:, 0:1]
    pull = jnp.broadcast_to(pull, tall).T[:, 0:1]
    conv = back[:, :per].reshape(peers * per, block).T
    gain = gain_ref[...]
    product = (query_ref[...].astype(F32) * conv).astype(BF16).astype(F32)
    put(0, product * scale * gain)
    gained = grad_ref[...].astype(F32) * gain
    grad = (gained * scale - product * pull).astype(BF16).astype(F32)
    put(1, grad * conv)
    for copy in copies:
        copy.wait()


def per_device(query, key, value, filters, gain, out_grad):
    peers = lax.axis_size(SEQ)
    groups = lax.axis_size(CHAN)
    line = lax.axis_size(LINE)
    plane = lax.axis_size(PLANE)
    block, wide = query.shape
    per = wide // peers
    width = float(wide * groups)
    table, twist = (jnp.asarray(part) for part in make_tables(peers, block, per))
    gain = gain.reshape(1, wide)
    home = (block, wide)
    owned = (peers, per, block)
    chunk = 2 * peers // line

    def exchange(array, axes):
        return lax.all_to_all(array, axes, split_axis=0, concat_axis=0, tiled=True)

    def merge(array, count, dtype, name):
        return call(
            merge_body, name, [(array, True)], [((count, chunk, block), dtype, True)]
        )[0]

    def dma(count):
        return pltpu.SemaphoreType.DMA((count,))

    loads = [key, value, filters, query, out_grad, gain, twist]
    key, value, filters, query, out_grad, gain, twist = call(
        load_body,
        "load",
        [(x, False) for x in loads],
        [(x.shape, x.dtype, True) for x in loads],
        [dma(len(loads))],
    )
    (packed,) = call(
        pack_body,
        "pack",
        [(x, True) for x in (key, value, filters, query, out_grad)],
        [((peers, 4 * per, block), BF16, True)],
        cost=pl.CostEstimate(flops=10**11, bytes_accessed=10**7, transcendentals=0),
    )
    packed = exchange(packed, SEQ)
    conv, values, gained, sums = call(
        convolve_body,
        "convolve",
        [(x, True) for x in (packed, gain, table, twist)],
        [
            (owned, BF16, True),
            ((2, wide, block), F32, True),
            (owned, F32, True),
            ((line, chunk, block), F32, True),
        ],
    )
    sums = exchange(sums, LINE)
    sums = exchange(merge(sums, plane, BF16, "merge_line"), PLANE)
    sums = exchange(merge(sums, line, F32, "merge_plane"), LINE)
    (back,) = call(
        functools.partial(correlate_body, width=width),
        "correlate",
        [(x, True) for x in (sums, packed, conv, gained, values, table, twist)],
        [((peers, 2 * per, block), BF16, True)],
    )
    back = exchange(back, SEQ)
    return tuple(
        call(
            functools.partial(finish_body, width=width),
            "finish",
            [(x, True) for x in (back, sums, key, value, query, out_grad, gain)],
            [(home, BF16, False)] * 4,
            [pltpu.VMEM((4,) + home, BF16), dma(4)],
        )
    )


def solution(mesh):
    cut = jax.sharding.Mesh(mesh.devices.reshape(4, 8, 8, 2, 2), SEQ + CHAN)
    tokens = P(SEQ, CHAN)
    return jax.shard_map(
        per_device,
        mesh=cut,
        in_specs=(tokens, tokens, tokens, P(CHAN, SEQ), P(CHAN), tokens),
        out_specs=(tokens, tokens, tokens, tokens),
        check_vma=False,
    )
```

```python
import functools

import jax
import jax.numpy as jnp
import numpy as np
from jax import lax
from jax.experimental import pallas as pl
from jax.experimental.pallas import tpu as pltpu
from jax.sharding import PartitionSpec as P

D = 8192
EPSILON = 1e-05

BF16 = jnp.bfloat16
F32 = jnp.float32

SEQ = ("y_lo", "z")
CHAN = ("x", "y_hi", "core")
LINE = ("y_lo", "y_hi", "core")
PLANE = ("x", "z")
VMEM_LIMIT = 24 << 20


def split_halves(table):
    high = table.astype(jnp.bfloat16)
    low = (table - high.astype(np.float64)).astype(jnp.bfloat16)
    return [high, low]


def make_tables(blocks, block, rows):
    length = blocks * block
    steps = np.arange(blocks)
    outer = np.exp(-2j * np.pi * np.outer(steps + 0.25, steps) / blocks)
    eye = np.eye(rows)
    first = np.kron(np.concatenate([outer.real, outer.imag], axis=0), eye)
    last = [np.kron(part.T, eye) / length for part in (outer.real, outer.imag)]
    twist = np.exp(-2j * np.pi * np.outer(steps + 0.25, np.arange(block)) / length)
    twist = np.concatenate([twist.real, twist.imag], axis=1).astype(np.float32)
    angle = 2 * np.pi * (np.outer(np.arange(block), np.arange(block)) % block) / block
    inner = np.block([[np.cos(angle), -np.sin(angle)], [np.sin(angle), np.cos(angle)]])
    parts = split_halves(first) + split_halves(inner)
    parts = parts + split_halves(last[0]) + split_halves(last[1])
    return (np.concatenate(parts, axis=0), twist)


class Table:
    def __init__(self, ref, twist_ref):
        self.ref = ref
        self.size = size = ref.shape[1]
        self.block = size // 2
        self.first = [(0, 2 * size), (2 * size, 2 * size)]
        self.inner = [(4 * size, size), (5 * size, size)]
        self.last = [[(6 * size, size), (7 * size, size)], [(8 * size, size), (9 * size, size)]]
        peers = twist_ref.shape[0]
        tall = (peers, size // peers, size)
        twist = jnp.broadcast_to(twist_ref[...].reshape(peers, 1, size), tall).reshape(size, size)
        self.turns = (twist[:, : self.block], twist[:, self.block :])

    def rows(self, span):
        return self.ref[span[0] : span[0] + span[1], :]


def halves(wide):
    high = wide.astype(BF16)
    low = (wide - high.astype(F32)).astype(BF16)
    return (high, low)


def mul(left, right, flip=False):
    dims = (((1,), (1 if flip else 0,)), ((), ()))
    return lax.dot_general(left, right, dims, preferred_element_type=F32)


def to_values(signal, table, turn_re, turn_im):
    rows, width = signal.shape
    block = table.block
    part = mul(table.rows(table.first[0]), signal) + mul(table.rows(table.first[1]), signal)
    turned = []
    for i in range(width // block):
        part_re = part[:rows, i * block : (i + 1) * block]
        part_im = part[rows:, i * block : (i + 1) * block]
        turned.append(
            jnp.concatenate(
                [part_re * turn_re - part_im * turn_im, part_re * turn_im + part_im * turn_re],
                axis=1,
            )
        )
    high, low = halves(jnp.concatenate(turned, axis=0))
    inner = [table.rows(span) for span in table.inner]
    values = mul(high, inner[0]) + (mul(high, inner[1]) + mul(low, inner[0]))
    return [
        (values[i * rows : (i + 1) * rows, :block], values[i * rows : (i + 1) * rows, block:])
        for i in range(width // block)
    ]


def to_signal(value_re, value_im, table, turn_re, turn_im):
    block = table.block
    high, low = halves(jnp.concatenate([value_re, value_im], axis=1))
    inner = [table.rows(span) for span in table.inner]
    back = mul(high, inner[0], True) + (mul(high, inner[1], True) + mul(low, inner[0], True))
    back_re, back_im = back[:, :block], back[:, block:]
    turned = (back_re * turn_re + back_im * turn_im, back_im * turn_re - back_re * turn_im)
    out = None
    for wide, (span_high, span_low) in zip(turned, table.last):
        high, low = halves(wide)
        both = mul(table.rows(span_high), jnp.concatenate([high, low], axis=1))
        term = both[:, :block] + (both[:, block:] + mul(table.rows(span_low), high))
        out = term if out is None else out + term
    return out


def call(body, name, args, outs, scratch=(), cost=None):
    whole = pl.BlockSpec(memory_space=pltpu.VMEM)
    apart = pl.BlockSpec(memory_space=pltpu.HBM)
    return pl.pallas_call(
        body,
        out_shape=[
            (pltpu.VMEM if keep else pltpu.HBM)(shape, dtype)
            for shape, dtype, keep in outs
        ],
        in_specs=[whole if keep else apart for _, keep in args],
        out_specs=[whole if keep else apart for _, _, keep in outs],
        scratch_shapes=list(scratch),
        cost_estimate=cost,
        compiler_params=pltpu.CompilerParams(vmem_limit_bytes=VMEM_LIMIT),
        name=name,
    )(
        *[
            pltpu.with_memory_space_constraint(x, pltpu.VMEM if keep else pltpu.HBM)
            for x, keep in args
        ]
    )


def load_body(*refs):
    count = len(refs) // 2
    sems = refs[-1]
    copies = [
        pltpu.make_async_copy(refs[i], refs[count + i], sems.at[i]) for i in range(count)
    ]
    for copy in copies:
        copy.start()
    for copy in copies:
        copy.wait()


def pack_body(key_ref, value_ref, filter_ref, query_ref, grad_ref, packed_ref):
    peers, rows, block = packed_ref.shape
    per = rows // 4

    def piece(wide):
        return wide.reshape(peers, per, block)

    query = piece(query_ref[...].astype(F32).T)
    grad = piece(grad_ref[...].astype(F32).T)
    packed_ref[:, 2 * per :, :] = jnp.concatenate([query, grad], axis=1).astype(BF16)
    source = (key_ref[...].astype(F32) * value_ref[...].astype(F32)).astype(BF16).astype(F32)
    taps = piece(filter_ref[...].astype(F32))
    packed_ref[:, : 2 * per, :] = jnp.concatenate([piece(source.T), taps], axis=1).astype(BF16)


def convolve_body(
    packed_ref, gain_ref, table_ref, twist_ref, out_ref, values_ref, gained_ref, sums_ref
):
    table = Table(table_ref, twist_ref)
    turns = table.turns
    peers, rows, block = packed_ref.shape
    per = rows // 4
    packed = packed_ref[:, : 2 * per, :].astype(F32)
    source = packed[:, :per].reshape(peers * per, block)
    taps = packed[:, per:].reshape(peers * per, block)
    signal = jnp.concatenate([source, taps], axis=1).astype(BF16)
    (src_re, src_im), (tap_re, tap_im) = to_values(signal, table, *turns)
    values_ref[0] = tap_re
    values_ref[1] = tap_im
    others = packed_ref[:, 2 * per :, :].astype(F32)
    query, grad = others[:, :per], others[:, per:]
    wide = gain_ref.shape[1]
    lane = lax.broadcasted_iota(jnp.int32, (per, wide), 1)
    channel = lax.broadcasted_iota(jnp.int32, (per, wide), 0) + per * lax.axis_index(SEQ)
    picked = jnp.where(lane == channel, jnp.broadcast_to(gain_ref[...], (per, wide)), 0.0)
    gained = grad * jnp.sum(picked, axis=1, keepdims=True)[None]
    gained_ref[...] = gained
    out = to_signal(
        src_re * tap_re - src_im * tap_im, src_re * tap_im + src_im * tap_re, table, *turns
    )
    conv = out.reshape(peers, per, block).astype(BF16)
    out_ref[...] = conv
    product = (query * conv.astype(F32)).astype(BF16).astype(F32)
    square = jnp.sum(product * product, axis=1, keepdims=True)
    cross = jnp.sum(gained * product, axis=1, keepdims=True)
    half = peers // 2
    sums_ref[...] = jnp.concatenate(
        [square[:half], square[half:], cross[:half], cross[half:]], axis=1
    )


def merge_body(sums_ref, out_ref):
    total = jnp.sum(sums_ref[...].astype(F32), axis=0, keepdims=True)
    out_ref[...] = jnp.broadcast_to(total, out_ref.shape).astype(out_ref.dtype)


def scales_of(square, cross, width):
    scale = lax.rsqrt(square / width + EPSILON)
    return (scale, cross * scale * scale * scale / width)


def correlate_body(
    sums_ref,
    packed_ref,
    conv_ref,
    gained_ref,
    values_ref,
    table_ref,
    twist_ref,
    out_ref,
    *,
    width,
):
    table = Table(table_ref, twist_ref)
    turns = table.turns
    peers, per, block = conv_ref.shape
    square = jnp.concatenate([sums_ref[:, 0:1, :], sums_ref[:, 1:2, :]], axis=0)
    cross = jnp.concatenate([sums_ref[:, 2:3, :], sums_ref[:, 3:4, :]], axis=0)
    scale, pull = scales_of(square, cross, width)
    conv = conv_ref[...].astype(F32)
    query = packed_ref[:, 2 * per :, :].astype(F32)[:, :per]
    product = (query * conv).astype(BF16).astype(F32)
    grad = (gained_ref[...] * scale - product * pull).astype(BF16).astype(F32)
    signal = (grad * query).reshape(peers * per, block).astype(BF16)
    ((sig_re, sig_im),) = to_values(signal, table, *turns)
    tap_re, tap_im = values_ref[0], values_ref[1]
    out = to_signal(
        sig_re * tap_re + sig_im * tap_im, sig_im * tap_re - sig_re * tap_im, table, *turns
    )
    spread = out.reshape(peers, per, block)
    out_ref[...] = jnp.concatenate([conv, spread], axis=1).astype(BF16)


def finish_body(
    back_ref,
    sums_ref,
    key_ref,
    value_ref,
    query_ref,
    grad_ref,
    gain_ref,
    normed_hbm,
    query_grad_hbm,
    key_grad_hbm,
    value_grad_hbm,
    outs_ref,
    sems,
    *,
    width,
):
    peers, rows, block = back_ref.shape
    per = rows // 2
    outs = [normed_hbm, query_grad_hbm, key_grad_hbm, value_grad_hbm]
    copies = [pltpu.make_async_copy(outs_ref.at[i], out, sems.at[i]) for i, out in enumerate(outs)]

    def put(i, wide):
        outs_ref[i] = wide.astype(BF16)
        copies[i].start()

    back = back_ref[...].astype(F32)
    spread = back[:, per:].reshape(peers * per, block).T
    put(2, spread * value_ref[...].astype(F32))
    put(3, spread * key_ref[...].astype(F32))
    half = peers // 2
    place = lax.axis_index(SEQ)
    mine = sums_ref[place % half]
    upper = place >= half
    square = jnp.where(upper, mine[1:2], mine[0:1])
    cross = jnp.where(upper, mine[3:4], mine[2:3])
    scale, pull = scales_of(square, cross, width)
    tall = (block, block)
    scale = jnp.broadcast_to(scale, tall).T[:, 0:1]
    pull = jnp.broadcast_to(pull, tall).T[:, 0:1]
    conv = back[:, :per].reshape(peers * per, block).T
    gain = gain_ref[...]
    product = (query_ref[...].astype(F32) * conv).astype(BF16).astype(F32)
    put(0, product * scale * gain)
    gained = grad_ref[...].astype(F32) * gain
    grad = (gained * scale - product * pull).astype(BF16).astype(F32)
    put(1, grad * conv)
    for copy in copies:
        copy.wait()


def per_device(query, key, value, filters, gain, out_grad):
    peers = lax.axis_size(SEQ)
    groups = lax.axis_size(CHAN)
    line = lax.axis_size(LINE)
    plane = lax.axis_size(PLANE)
    block, wide = query.shape
    per = wide // peers
    width = float(wide * groups)
    table, twist = (jnp.asarray(part) for part in make_tables(peers, block, per))
    gain = gain.reshape(1, wide)
    home = (block, wide)
    owned = (peers, per, block)
    chunk = 2 * peers // line

    def exchange(array, axes):
        return lax.all_to_all(array, axes, split_axis=0, concat_axis=0, tiled=True)

    def merge(array, count, dtype, name):
        return call(
            merge_body, name, [(array, True)], [((count, chunk, block), dtype, True)]
        )[0]

    def dma(count):
        return pltpu.SemaphoreType.DMA((count,))

    loads = [key, value, filters, query, out_grad, gain, twist]
    key, value, filters, query, out_grad, gain, twist = call(
        load_body,
        "load",
        [(x, False) for x in loads],
        [(x.shape, x.dtype, True) for x in loads],
        [dma(len(loads))],
    )
    (packed,) = call(
        pack_body,
        "pack",
        [(x, True) for x in (key, value, filters, query, out_grad)],
        [((peers, 4 * per, block), BF16, True)],
        cost=pl.CostEstimate(flops=10**11, bytes_accessed=10**7, transcendentals=0),
    )
    packed = exchange(packed, SEQ)
    conv, values, gained, sums = call(
        convolve_body,
        "convolve",
        [(x, True) for x in (packed, gain, table, twist)],
        [
            (owned, BF16, True),
            ((2, wide, block), F32, True),
            (owned, F32, True),
            ((line, chunk, block), F32, True),
        ],
    )
    sums = exchange(sums, LINE)
    sums = exchange(merge(sums, plane, BF16, "merge_line"), PLANE)
    sums = exchange(merge(sums, line, F32, "merge_plane"), LINE)
    (back,) = call(
        functools.partial(correlate_body, width=width),
        "correlate",
        [(x, True) for x in (sums, packed, conv, gained, values, table, twist)],
        [((peers, 2 * per, block), BF16, True)],
    )
    back = exchange(back, SEQ)
    return tuple(
        call(
            functools.partial(finish_body, width=width),
            "finish",
            [(x, True) for x in (back, sums, key, value, query, out_grad, gain)],
            [(home, BF16, False)] * 4,
            [pltpu.VMEM((4,) + home, BF16), dma(4)],
        )
    )


def solution(mesh):
    cut = jax.sharding.Mesh(mesh.devices.reshape(4, 8, 8, 2, 2), SEQ + CHAN)
    tokens = P(SEQ, CHAN)
    return jax.shard_map(
        per_device,
        mesh=cut,
        in_specs=(tokens, tokens, tokens, P(CHAN, SEQ), P(CHAN), tokens),
        out_specs=(tokens, tokens, tokens, tokens),
        check_vma=False,
    )
```
